32 devices in a mesh: groups: 2 (over x), tok: 16 (over z, y, core).
Axes of the slice: x: 2, y: 2, z: 4, core: 2. Of those that a mesh axis runs over, the one named last changes fastest.
Arguments:
- features: bfloat16 [16, 1024, 768], P('tok', 'groups'), parts along dimension 1, may hold values from -6 to 6
- w_up: bfloat16 [2, 16, 768, 1536], P(None, 'tok'), may hold values from -0.21875 to 0.21875
- w_down: bfloat16 [2, 16, 1536, 768], P(None, 'tok'), may hold values from -0.109375 to 0.109375
- gains: float32 [2, 8, 768], replicated, may hold values from 0.1 to 1.9
Outputs:
- result: bfloat16 [16, 1024, 768], P('tok', 'groups'), parts along dimension 1
The draws below stay inside these ranges and needn't reach their ends.
There are 2 independent parts, one for each index of `groups`. The reference program is written for one: setup_inputs(seed, part) draws one part's arguments, and reference() takes and returns one part's arrays. A program takes and returns all parts, laid end to end along the dimension named above; an argument that names none is the same for every part. Nothing has to cross between parts.
All inputs are finite; a program needn't handle non-finite values.
Results may differ from the reference program's by a relative error of at most 0.0059.
Values may be sent and summed in bfloat16 or wider, within the bound.
No kernel may reach another device: no remote copies, remote signals or barrier semaphores. Data moves between devices by JAX's collectives and lax.ppermute only.
A program may use at most 64 MiB of HBM per device.

```python
import jax
import jax.numpy as jnp
from jax import lax

D = 768
FF = 3072
LAYERS = 2
ROWS = 1024
TOKENS = 8
HW = 96


def block_scale(rng, shape, cuts, least, largest):
    def one(axis_at, shards_of):
        steps = jax.random.uniform(jax.random.fold_in(jax.random.fold_in(rng, 6), axis_at), (shards_of,), jnp.float32, least / len(cuts), largest / len(cuts))
        return jnp.repeat(jnp.exp(steps), shape[axis_at] // shards_of).reshape((-1,) + (1,) * (len(shape) - axis_at - 1))

    loudness = one(*cuts[0])
    for cut in cuts[1:]:
        loudness = loudness * one(*cut)
    return loudness


def normal_values(rng, dims, width, reach, split=(), kind=jnp.bfloat16):
    entries = jax.random.normal(rng, dims, jnp.float32) * width
    if len(split) > 0:
        entries = block_scale(rng, dims, split, -0.22, 0.18) * entries
    return jnp.clip(entries, min=-reach, max=reach).astype(kind)


def setup_inputs(seed: int = 0, part: int = 0) -> dict:
    splits = jax.random.split(jax.random.key(seed), 5)
    part_keys = jax.random.split(jax.random.fold_in(splits[4], part), 5)
    return {
        "features": normal_values(part_keys[0], (2 * TOKENS, ROWS // 2, D), 1.0, 6.0, ((0, 16),)),
        "w_up": normal_values(splits[1], (LAYERS, 2 * TOKENS, D, FF // 2), D ** -0.5, 0.21875, ((1, 16),)),
        "w_down": normal_values(splits[2], (LAYERS, 2 * TOKENS, FF // 2, D), FF ** -0.5, 0.109375, ((1, 16),)),
        "gains": jnp.clip(1.0 + 0.18 * jax.random.normal(splits[3], (LAYERS, TOKENS, D), jnp.float32), 0.1, 1.9),
    }


def token_layer(args):
    mixed, w_first, w_second, gain = args
    values = mixed.astype(jnp.float32)
    scale = lax.rsqrt(lax.optimization_barrier(jnp.mean(values * values, axis=-1, keepdims=True)) + 1e-06)
    normed = (values * scale * gain).astype(jnp.bfloat16)
    hidden = jax.nn.gelu(jnp.dot(normed, w_first, preferred_element_type=jnp.float32), approximate=True).astype(jnp.bfloat16)
    update = jnp.dot(hidden, w_second, preferred_element_type=jnp.float32)
    return (values + update).astype(jnp.bfloat16)

def reference(features, w_up, w_down, gains):
    half_rows = ROWS // 2
    state = features.reshape(TOKENS, ROWS, D)
    for layer in range(LAYERS):
        mixed = state.reshape(TOKENS, ROWS, TOKENS, HW).transpose(2, 1, 0, 3).reshape(TOKENS, ROWS, D)
        w_first = w_up[layer].reshape(TOKENS, 2, D, FF // 2).transpose(0, 2, 1, 3).reshape(TOKENS, D, FF)
        w_second = w_down[layer].reshape(TOKENS, FF, D)
        state = lax.map(token_layer, (mixed, w_first, w_second, gains[layer]))
    return state.reshape(2 * TOKENS, half_rows, D)
```

```python
import functools

import jax
import jax.numpy as jnp
from jax import lax
from jax.experimental import pallas as pl
from jax.experimental.pallas import tpu as pltpu
from jax.sharding import PartitionSpec as P

EPS = 1e-06
CUBIC = 0.044715
ROOT = 0.7978845608028654
VMEM_LIMIT = 16 << 20
IN_VMEM = pl.BlockSpec(memory_space=pltpu.VMEM)


def partner(token, step, tokens):
    return token ^ step


def store_blocks(turned_ref, out_refs):
    tokens = len(out_refs)
    height = out_refs[0].shape[0]
    token = lax.axis_index("tok") // 2
    for step, out_ref in enumerate(out_refs):
        start = pl.multiple_of(partner(token, step, tokens) * height, height)
        out_ref[...] = turned_ref[pl.ds(start, height), :]


def split_kernel(x_ref, *refs):
    *out_refs, turned_ref = refs
    turned_ref[...] = x_ref[0].T
    store_blocks(turned_ref, out_refs)


def split(features, tokens):
    _, rows, width = features.shape
    height = width // tokens
    return pl.pallas_call(
        split_kernel,
        in_specs=[IN_VMEM],
        out_specs=[IN_VMEM] * tokens,
        out_shape=[jax.ShapeDtypeStruct((height, rows), features.dtype)] * tokens,
        scratch_shapes=[pltpu.VMEM((width, rows), features.dtype)],
        compiler_params=pltpu.CompilerParams(vmem_limit_bytes=VMEM_LIMIT),
        cost_estimate=pl.CostEstimate(
            flops=20000000000, bytes_accessed=4 * rows * width, transcendentals=0
        ),
    )(features)


def gelu(v):
    half = 0.5 * v
    return half + half * jnp.tanh(v * (ROOT + (ROOT * CUBIC) * (v * v)))


def ffn_kernel(tokens, layer, last, tile, *refs):
    block_refs = refs[:tokens]
    gain_ref, up_a, up_b, down_a, down_b = refs[tokens : tokens + 5]
    out_refs = refs[tokens + 5 : -3]
    turned_ref, normed_ref, total_ref = refs[-3:]
    height = block_refs[0].shape[0]
    token = lax.axis_index("tok") // 2
    for step, ref in enumerate(block_refs):
        start = pl.multiple_of(partner(token, step, tokens) * height, height)
        turned_ref[pl.ds(start, height), :] = ref[...]
    values = turned_ref[...].T.astype(jnp.float32)
    mean = jnp.mean(values * values, axis=-1, keepdims=True)
    normed = values * lax.rsqrt(mean + EPS) * gain_ref[layer, pl.ds(token, 1), :]
    normed_ref[...] = normed.astype(jnp.bfloat16)
    total_ref[...] = values
    for start in range(0, up_a.shape[-1], tile):
        part = slice(start, start + tile)
        normed = normed_ref[...]
        update = None
        for up, down in ((up_a, down_a), (up_b, down_b)):
            hidden = jnp.dot(
                normed, up[layer, 0, :, part], preferred_element_type=jnp.float32
            )
            hidden = gelu(hidden).astype(jnp.bfloat16)
            term = jnp.dot(
                hidden, down[layer, 0, part, :], preferred_element_type=jnp.float32
            )
            update = term if update is None else update + term
        total_ref[...] += update
    state = total_ref[...].astype(jnp.bfloat16)
    if last:
        out_refs[0][0] = state
    else:
        turned_ref[...] = state.T
        store_blocks(turned_ref, out_refs)


def ffn(blocks, gains, ups, downs, layer, last):
    tokens = len(blocks)
    height, rows = blocks[0].shape
    width = height * tokens
    hidden = ups[0].shape[-1]
    tile = 768 if hidden % 768 == 0 else hidden
    if last:
        out_shape = [jax.ShapeDtypeStruct((1, rows, width), jnp.bfloat16)]
    else:
        out_shape = [jax.ShapeDtypeStruct((height, rows), jnp.bfloat16)] * tokens
    return pl.pallas_call(
        functools.partial(ffn_kernel, tokens, layer, last, tile),
        in_specs=[IN_VMEM] * (tokens + 5),
        out_specs=[IN_VMEM] * len(out_shape),
        out_shape=out_shape,
        scratch_shapes=[
            pltpu.VMEM((width, rows), jnp.bfloat16),
            pltpu.VMEM((rows, width), jnp.bfloat16),
            pltpu.VMEM((rows, width), jnp.float32),
        ],
        compiler_params=pltpu.CompilerParams(vmem_limit_bytes=VMEM_LIMIT),
        cost_estimate=pl.CostEstimate(
            flops=8 * rows * width * hidden,
            bytes_accessed=8 * width * hidden + 4 * rows * width,
            transcendentals=2 * rows * hidden,
        ),
    )(*blocks, gains, *ups, *downs)


def order(tokens):
    half = tokens // 2
    return list(range(half, tokens)) + list(range(1, half))


def exchange(blocks):
    tokens = len(blocks)
    received = [blocks[0]] + [None] * (tokens - 1)
    for step in order(tokens):
        pairs = [
            (2 * t + h, 2 * partner(t, step, tokens) + h)
            for t in range(tokens)
            for h in range(2)
        ]
        received[step] = lax.ppermute(blocks[step], "tok", pairs)
    return received


def shards(features, w_up, w_down, gains):
    count = lax.axis_size("tok")
    tokens = count // 2
    pairs = [(i, i ^ 1) for i in range(count)]
    ups = (w_up, lax.ppermute(w_up, "tok", pairs))
    downs = (w_down, lax.ppermute(w_down, "tok", pairs))
    blocks = split(features, tokens)
    layers = w_up.shape[0]
    for layer in range(layers):
        blocks = exchange(blocks)
        blocks = ffn(blocks, gains, ups, downs, layer, layer == layers - 1)
    return blocks[0]


def solution(mesh):
    placed = (P("tok", "groups", None), P(None, "tok", None, None), P(None, "tok", None, None), P())
    return jax.shard_map(
        shards, mesh=mesh, in_specs=placed, out_specs=P("tok", "groups", None), check_vma=False
    )
```

```python
import functools

import jax
import jax.numpy as jnp
from jax import lax
from jax.experimental import pallas as pl
from jax.experimental.pallas import tpu as pltpu
from jax.sharding import PartitionSpec as P

EPS = 1e-06
CUBIC = 0.044715
ROOT = 0.7978845608028654
VMEM_LIMIT = 16 << 20
TILE = 768
IN_VMEM = pl.BlockSpec(memory_space=pltpu.VMEM)


def params():
    return pltpu.CompilerParams(vmem_limit_bytes=VMEM_LIMIT)


def order(tokens):
    half, quarter = tokens // 2, tokens // 4
    near, far = list(range(1, half)), list(range(half, half + quarter))
    mixed = []
    while near or far:
        mixed += near[:1] + far[:1]
        near, far = near[1:], far[1:]
    return mixed + list(range(half + quarter, tokens))


def this_token():
    return lax.axis_index("tok") // 2


def block_rows(step, height):
    return pl.ds(pl.multiple_of((this_token() ^ step) * height, height), height)


def store_blocks(steps, turned_ref, out_refs):
    for step, out_ref in zip(steps, out_refs):
        out_ref[...] = turned_ref[block_rows(step, out_ref.shape[0]), :]


def load_blocks(steps, block_refs, turned_ref):
    for step, ref in zip(steps, block_refs):
        turned_ref[block_rows(step, ref.shape[0]), :] = ref[...]


def quarter_rows(tokens, width, which):
    quarter = this_token() // (tokens // 4) ^ which
    return pl.ds(pl.multiple_of(quarter * (width // 4), width // 4), width // 4)


def split_kernel(tokens, x_ref, *refs):
    *out_refs, turned_ref = refs
    turned_ref[...] = x_ref[0].T
    store_blocks(range(tokens), turned_ref, out_refs)


def split(features, tokens):
    _, rows, width = features.shape
    block = jax.ShapeDtypeStruct((width // tokens, rows), features.dtype)
    return pl.pallas_call(
        functools.partial(split_kernel, tokens),
        in_specs=[IN_VMEM],
        out_specs=[IN_VMEM] * tokens,
        out_shape=[block] * tokens,
        scratch_shapes=[pltpu.VMEM((width, rows), features.dtype)],
        compiler_params=params(),
        cost_estimate=pl.CostEstimate(
            flops=20000000000, bytes_accessed=4 * rows * width, transcendentals=0
        ),
    )(features)


def gelu(v):
    half = 0.5 * v
    return half + half * jnp.tanh(v * (ROOT + (ROOT * CUBIC) * (v * v)))


def gained(tokens, which, turned_ref, column_ref):
    width = turned_ref.shape[0]
    rows = quarter_rows(tokens, width, which)
    values = turned_ref[rows, :].astype(jnp.float32) * column_ref[rows, :1]
    return values.astype(jnp.bfloat16).T


def gain_column(layer, gain_ref, column_ref):
    gain = gain_ref[layer, pl.ds(this_token(), 1), :]
    column_ref[...] = jnp.broadcast_to(gain, column_ref.shape[::-1]).T


def tiles(size):
    tile = TILE if size % TILE == 0 else size
    return [slice(start, start + tile) for start in range(0, size, tile)]


def early_kernel(tokens, steps, layer, *refs):
    count = len(steps)
    block_refs = refs[:count]
    gain_ref, *up_refs, out_ref, turned_ref, column_ref = refs[count:]
    width = turned_ref.shape[0]
    load_blocks(steps, block_refs, turned_ref)
    gain_column(layer, gain_ref, column_ref)
    parts = [
        gained(tokens, which, turned_ref, column_ref)
        for which in range(3)
    ]
    for half, up_ref in enumerate(up_refs):
        for tile in tiles(up_ref.shape[-1]):
            total = None
            for which, part in enumerate(parts):
                rows = quarter_rows(tokens, width, which)
                term = jnp.dot(
                    part,
                    up_ref[layer, 0, rows, tile],
                    preferred_element_type=jnp.float32,
                )
                total = term if total is None else total + term
            out_ref[half, :, tile] = total


def early(blocks, gains, ups, layer):
    height, rows = blocks[0].shape
    width, hidden = ups[0].shape[2:]
    tokens = width // height
    steps = [step for step in [*order(tokens), 0] if step < tokens * 3 // 4]
    return pl.pallas_call(
        functools.partial(early_kernel, tokens, steps, layer),
        in_specs=[IN_VMEM] * (len(steps) + 3),
        out_specs=IN_VMEM,
        out_shape=jax.ShapeDtypeStruct((2, rows, hidden), jnp.float32),
        scratch_shapes=[
            pltpu.VMEM((width, rows), jnp.bfloat16),
            pltpu.VMEM((width, 128), jnp.float32),
        ],
        compiler_params=params(),
        cost_estimate=pl.CostEstimate(
            flops=3 * rows * width * hidden,
            bytes_accessed=4 * width * hidden,
            transcendentals=0,
        ),
    )(*[blocks[step] for step in steps], gains, *ups)


def late_kernel(tokens, steps, layer, last, *refs):
    count = len(steps)
    block_refs = refs[:count]
    early_ref, gain_ref, up_a, up_b, down_a, down_b = refs[count : count + 6]
    out_refs = refs[count + 6 : -3]
    turned_ref, column_ref, total_ref = refs[-3:]
    width = turned_ref.shape[0]
    load_blocks(steps, block_refs, turned_ref)
    gain_column(layer, gain_ref, column_ref)
    part = gained(tokens, 3, turned_ref, column_ref)
    values = turned_ref[...].T.astype(jnp.float32)
    mean = jnp.mean(values * values, axis=-1, keepdims=True)
    scale = lax.rsqrt(mean + EPS)
    total_ref[...] = values
    for half, (up, down) in enumerate(((up_a, down_a), (up_b, down_b))):
        for tile in tiles(up.shape[-1]):
            rows = quarter_rows(tokens, width, 3)
            hidden = jnp.dot(
                part, up[layer, 0, rows, tile], preferred_element_type=jnp.float32
            )
            hidden = gelu((hidden + early_ref[half, :, tile]) * scale)
            total_ref[...] += jnp.dot(
                hidden.astype(jnp.bfloat16),
                down[layer, 0, tile, :],
                preferred_element_type=jnp.float32,
            )
    state = total_ref[...].astype(jnp.bfloat16)
    if last:
        out_refs[0][0] = state
    else:
        turned_ref[...] = state.T
        store_blocks(range(tokens), turned_ref, out_refs)


def late(blocks, begun, gains, ups, downs, layer, last):
    height, rows = blocks[0].shape
    width, hidden = ups[0].shape[2:]
    tokens = width // height
    steps = [0, *order(tokens)]
    if last:
        out_shape = [jax.ShapeDtypeStruct((1, rows, width), jnp.bfloat16)]
    else:
        out_shape = [jax.ShapeDtypeStruct((height, rows), jnp.bfloat16)] * tokens
    return pl.pallas_call(
        functools.partial(late_kernel, tokens, steps, layer, last),
        in_specs=[IN_VMEM] * (tokens + 6),
        out_specs=[IN_VMEM] * len(out_shape),
        out_shape=out_shape,
        scratch_shapes=[
            pltpu.VMEM((width, rows), jnp.bfloat16),
            pltpu.VMEM((width, 128), jnp.float32),
            pltpu.VMEM((rows, width), jnp.float32),
        ],
        compiler_params=params(),
        cost_estimate=pl.CostEstimate(
            flops=5 * rows * width * hidden,
            bytes_accessed=8 * width * hidden,
            transcendentals=2 * rows * hidden,
        ),
    )(*[blocks[step] for step in steps], begun, gains, *ups, *downs)


def exchange(blocks):
    tokens = len(blocks)
    received = [blocks[0]] + [None] * (tokens - 1)
    for step in order(tokens):
        pairs = [
            (2 * t + h, 2 * (t ^ step) + h) for t in range(tokens) for h in range(2)
        ]
        received[step] = lax.ppermute(blocks[step], "tok", pairs)
    return received


def shards(features, w_up, w_down, gains):
    count = lax.axis_size("tok")
    tokens = count // 2
    pairs = [(i, i ^ 1) for i in range(count)]
    ups = (w_up, lax.ppermute(w_up, "tok", pairs))
    downs = (w_down, lax.ppermute(w_down, "tok", pairs))
    blocks = split(features, tokens)
    layers = w_up.shape[0]
    for layer in range(layers):
        blocks = exchange(blocks)
        begun = early(blocks, gains, ups, layer)
        blocks = late(blocks, begun, gains, ups, downs, layer, layer == layers - 1)
    return blocks[0]


def solution(mesh):
    placed = (P("tok", "groups", None), P(None, "tok", None, None), P(None, "tok", None, None), P())
    return jax.shard_map(
        shards, mesh=mesh, in_specs=placed, out_specs=P("tok", "groups", None), check_vma=False
    )
```

```python
import functools

import jax
import jax.numpy as jnp
from jax import lax
from jax.experimental import pallas as pl
from jax.experimental.pallas import tpu as pltpu
from jax.sharding import PartitionSpec as P

EPS = 1e-06
CUBIC = 0.044715
ROOT = 0.7978845608028654
VMEM_LIMIT = 16 << 20
TILE = 768
IN_VMEM = pl.BlockSpec(memory_space=pltpu.VMEM)


def params():
    return pltpu.CompilerParams(vmem_limit_bytes=VMEM_LIMIT)


def order(tokens, layer):
    half, quarter = tokens // 2, tokens // 4
    near, far = list(range(1, half)), list(range(half, half + quarter))
    if layer:
        near.sort(key=lambda step: step != 2)
        near, far = far, near
    mixed = []
    while near or far:
        mixed += near[:1] + far[:1]
        near, far = near[1:], far[1:]
    return mixed + list(range(half + quarter, tokens))


def this_token():
    return lax.axis_index("tok") // 2


def block_rows(step, height):
    return pl.ds(pl.multiple_of((this_token() ^ step) * height, height), height)


def store_blocks(steps, turned_ref, out_refs):
    for step, out_ref in zip(steps, out_refs):
        out_ref[...] = turned_ref[block_rows(step, out_ref.shape[0]), :]


def load_blocks(steps, block_refs, turned_ref):
    for step, ref in zip(steps, block_refs):
        turned_ref[block_rows(step, ref.shape[0]), :] = ref[...]


def quarter_rows(tokens, width, which):
    quarter = this_token() // (tokens // 4) ^ which
    return pl.ds(pl.multiple_of(quarter * (width // 4), width // 4), width // 4)


def split_kernel(tokens, x_ref, *refs):
    *out_refs, turned_ref = refs
    turned_ref[...] = x_ref[0].T
    store_blocks(range(tokens), turned_ref, out_refs)


def split(features, tokens):
    _, rows, width = features.shape
    block = jax.ShapeDtypeStruct((width // tokens, rows), features.dtype)
    return pl.pallas_call(
        functools.partial(split_kernel, tokens),
        in_specs=[IN_VMEM],
        out_specs=[IN_VMEM] * tokens,
        out_shape=[block] * tokens,
        scratch_shapes=[pltpu.VMEM((width, rows), features.dtype)],
        compiler_params=params(),
        cost_estimate=pl.CostEstimate(
            flops=20000000000, bytes_accessed=4 * rows * width, transcendentals=0
        ),
    )(features)


def gelu(v):
    half = 0.5 * v
    return half + half * jnp.tanh(v * (ROOT + (ROOT * CUBIC) * (v * v)))


def gained(tokens, which, turned_ref, column_ref):
    width = turned_ref.shape[0]
    rows = quarter_rows(tokens, width, which)
    values = turned_ref[rows, :].astype(jnp.float32) * column_ref[rows, :1]
    return values.astype(jnp.bfloat16).T


def gain_column(layer, gain_ref, column_ref):
    gain = gain_ref[layer, pl.ds(this_token(), 1), :]
    column_ref[...] = jnp.broadcast_to(gain, column_ref.shape[::-1]).T


def tiles(size):
    tile = TILE if size % TILE == 0 else size
    return [slice(start, start + tile) for start in range(0, size, tile)]


def early_kernel(tokens, steps, layer, *refs):
    count = len(steps)
    block_refs = refs[:count]
    gain_ref, *up_refs, out_ref, turned_ref, column_ref = refs[count:]
    width = turned_ref.shape[0]
    load_blocks(steps, block_refs, turned_ref)
    gain_column(layer, gain_ref, column_ref)
    parts = [
        gained(tokens, which, turned_ref, column_ref)
        for which in range(3)
    ]
    for half, up_ref in enumerate(up_refs):
        for tile in tiles(up_ref.shape[-1]):
            total = None
            for which, part in enumerate(parts):
                rows = quarter_rows(tokens, width, which)
                term = jnp.dot(
                    part,
                    up_ref[layer, 0, rows, tile],
                    preferred_element_type=jnp.float32,
                )
                total = term if total is None else total + term
            out_ref[half, :, tile] = total


def early(blocks, gains, ups, layer):
    height, rows = blocks[0].shape
    width, hidden = ups[0].shape[2:]
    tokens = width // height
    steps = [step for step in [*order(tokens, layer), 0] if step < tokens * 3 // 4]
    return pl.pallas_call(
        functools.partial(early_kernel, tokens, steps, layer),
        in_specs=[IN_VMEM] * (len(steps) + 3),
        out_specs=IN_VMEM,
        out_shape=jax.ShapeDtypeStruct((2, rows, hidden), jnp.float32),
        scratch_shapes=[
            pltpu.VMEM((width, rows), jnp.bfloat16),
            pltpu.VMEM((width, 128), jnp.float32),
        ],
        compiler_params=params(),
        cost_estimate=pl.CostEstimate(
            flops=3 * rows * width * hidden,
            bytes_accessed=4 * width * hidden,
            transcendentals=0,
        ),
    )(*[blocks[step] for step in steps], gains, *ups)


def late_kernel(tokens, steps, layer, last, *refs):
    count = len(steps)
    block_refs = refs[:count]
    early_ref, gain_ref, up_a, up_b, down_a, down_b = refs[count : count + 6]
    out_refs = refs[count + 6 : -3]
    turned_ref, column_ref, total_ref = refs[-3:]
    width = turned_ref.shape[0]
    load_blocks(steps, block_refs, turned_ref)
    gain_column(layer, gain_ref, column_ref)
    part = gained(tokens, 3, turned_ref, column_ref)
    values = turned_ref[...].T.astype(jnp.float32)
    mean = jnp.mean(values * values, axis=-1, keepdims=True)
    scale = lax.rsqrt(mean + EPS)
    total_ref[...] = values
    for half, (up, down) in enumerate(((up_a, down_a), (up_b, down_b))):
        for tile in tiles(up.shape[-1]):
            rows = quarter_rows(tokens, width, 3)
            hidden = jnp.dot(
                part, up[layer, 0, rows, tile], preferred_element_type=jnp.float32
            )
            hidden = gelu((hidden + early_ref[half, :, tile]) * scale)
            total_ref[...] += jnp.dot(
                hidden.astype(jnp.bfloat16),
                down[layer, 0, tile, :],
                preferred_element_type=jnp.float32,
            )
    state = total_ref[...].astype(jnp.bfloat16)
    if last:
        out_refs[0][0] = state
    else:
        turned_ref[...] = state.T
        store_blocks(range(tokens), turned_ref, out_refs)


def late(blocks, begun, gains, ups, downs, layer, last):
    height, rows = blocks[0].shape
    width, hidden = ups[0].shape[2:]
    tokens = width // height
    steps = [0, *order(tokens, layer)]
    if last:
        out_shape = [jax.ShapeDtypeStruct((1, rows, width), jnp.bfloat16)]
    else:
        out_shape = [jax.ShapeDtypeStruct((height, rows), jnp.bfloat16)] * tokens
    return pl.pallas_call(
        functools.partial(late_kernel, tokens, steps, layer, last),
        in_specs=[IN_VMEM] * (tokens + 6),
        out_specs=[IN_VMEM] * len(out_shape),
        out_shape=out_shape,
        scratch_shapes=[
            pltpu.VMEM((width, rows), jnp.bfloat16),
            pltpu.VMEM((width, 128), jnp.float32),
            pltpu.VMEM((rows, width), jnp.float32),
        ],
        compiler_params=params(),
        cost_estimate=pl.CostEstimate(
            flops=5 * rows * width * hidden,
            bytes_accessed=8 * width * hidden,
            transcendentals=2 * rows * hidden,
        ),
    )(*[blocks[step] for step in steps], begun, gains, *ups, *downs)


def exchange(blocks, layer):
    tokens = len(blocks)
    received = [blocks[0]] + [None] * (tokens - 1)
    for step in order(tokens, layer):
        pairs = [
            (2 * t + h, 2 * (t ^ step) + h) for t in range(tokens) for h in range(2)
        ]
        received[step] = lax.ppermute(blocks[step], "tok", pairs)
    return received


def shards(features, w_up, w_down, gains):
    count = lax.axis_size("tok")
    tokens = count // 2
    pairs = [(i, i ^ 1) for i in range(count)]
    ups = (w_up, lax.ppermute(w_up, "tok", pairs))
    downs = (w_down, lax.ppermute(w_down, "tok", pairs))
    blocks = split(features, tokens)
    layers = w_up.shape[0]
    for layer in range(layers):
        blocks = exchange(blocks, layer)
        begun = early(blocks, gains, ups, layer)
        blocks = late(blocks, begun, gains, ups, downs, layer, layer == layers - 1)
    return blocks[0]


def solution(mesh):
    placed = (P("tok", "groups", None), P(None, "tok", None, None), P(None, "tok", None, None), P())
    return jax.shard_map(
        shards, mesh=mesh, in_specs=placed, out_specs=P("tok", "groups", None), check_vma=False
    )
```

```python
import functools

import jax
import jax.numpy as jnp
from jax import lax
from jax.experimental import pallas as pl
from jax.experimental.pallas import tpu as pltpu
from jax.sharding import PartitionSpec as P

EPS = 1e-06
CUBIC = 0.044715
ROOT = 0.7978845608028654
VMEM_LIMIT = 16 << 20
TILE = 768
IN_VMEM = pl.BlockSpec(memory_space=pltpu.VMEM)


def params():
    return pltpu.CompilerParams(vmem_limit_bytes=VMEM_LIMIT)


def order(tokens, layer):
    half, quarter = tokens // 2, tokens // 4
    near = list(range(1, half))
    third, fourth = (
        list(range(start, start + quarter)) for start in (half, half + quarter)
    )
    if layer == 0:
        first, second, latest = near, fourth, third
    else:
        near.sort(key=lambda step: step != 2)
        first, second, latest = third, near, fourth
    mixed = []
    while first or second:
        mixed += first[:1] + second[:1]
        first, second = first[1:], second[1:]
    return mixed + latest


def this_token():
    return lax.axis_index("tok") // 2


def block_rows(step, height):
    return pl.ds(pl.multiple_of((this_token() ^ step) * height, height), height)


def store_blocks(steps, turned_ref, out_refs):
    for step, out_ref in zip(steps, out_refs):
        out_ref[...] = turned_ref[block_rows(step, out_ref.shape[0]), :]


def load_blocks(steps, block_refs, turned_ref):
    for step, ref in zip(steps, block_refs):
        turned_ref[block_rows(step, ref.shape[0]), :] = ref[...]


def quarter_rows(tokens, width, which):
    quarter = this_token() // (tokens // 4) ^ which
    return pl.ds(pl.multiple_of(quarter * (width // 4), width // 4), width // 4)


def split_kernel(tokens, x_ref, *refs):
    *out_refs, turned_ref = refs
    turned_ref[...] = x_ref[0].T
    store_blocks(range(tokens), turned_ref, out_refs)


def split(features, tokens):
    _, rows, width = features.shape
    block = jax.ShapeDtypeStruct((width // tokens, rows), features.dtype)
    return pl.pallas_call(
        functools.partial(split_kernel, tokens),
        in_specs=[IN_VMEM],
        out_specs=[IN_VMEM] * tokens,
        out_shape=[block] * tokens,
        scratch_shapes=[pltpu.VMEM((width, rows), features.dtype)],
        compiler_params=params(),
        cost_estimate=pl.CostEstimate(
            flops=20000000000, bytes_accessed=4 * rows * width, transcendentals=0
        ),
    )(features)


def gelu(v):
    half = 0.5 * v
    return half + half * jnp.tanh(v * (ROOT + (ROOT * CUBIC) * (v * v)))


def quarters(tokens, layer):
    latest = order(tokens, layer)[-1] // (tokens // 4)
    return [which for which in range(4) if which != latest] + [latest]


def gained(tokens, which, turned_ref, column_ref):
    width = turned_ref.shape[0]
    rows = quarter_rows(tokens, width, which)
    values = turned_ref[rows, :].astype(jnp.float32) * column_ref[rows, :1]
    return values.astype(jnp.bfloat16).T


def gain_column(layer, gain_ref, column_ref):
    gain = gain_ref[layer, pl.ds(this_token(), 1), :]
    column_ref[...] = jnp.broadcast_to(gain, column_ref.shape[::-1]).T


def tiles(size):
    tile = TILE if size % TILE == 0 else size
    return [slice(start, start + tile) for start in range(0, size, tile)]


def early_kernel(tokens, steps, layer, *refs):
    count = len(steps)
    block_refs = refs[:count]
    gain_ref, *up_refs, out_ref, turned_ref, column_ref = refs[count:]
    width = turned_ref.shape[0]
    load_blocks(steps, block_refs, turned_ref)
    gain_column(layer, gain_ref, column_ref)
    parts = [
        gained(tokens, which, turned_ref, column_ref)
        for which in quarters(tokens, layer)[:3]
    ]
    for half, up_ref in enumerate(up_refs):
        for tile in tiles(up_ref.shape[-1]):
            total = None
            for which, part in zip(quarters(tokens, layer), parts):
                rows = quarter_rows(tokens, width, which)
                term = jnp.dot(
                    part,
                    up_ref[layer, 0, rows, tile],
                    preferred_element_type=jnp.float32,
                )
                total = term if total is None else total + term
            out_ref[half, :, tile] = total


def early(blocks, gains, ups, layer):
    height, rows = blocks[0].shape
    width, hidden = ups[0].shape[2:]
    tokens = width // height
    steps = [*order(tokens, layer)[: -(tokens // 4)], 0]
    return pl.pallas_call(
        functools.partial(early_kernel, tokens, steps, layer),
        in_specs=[IN_VMEM] * (len(steps) + 3),
        out_specs=IN_VMEM,
        out_shape=jax.ShapeDtypeStruct((2, rows, hidden), jnp.float32),
        scratch_shapes=[
            pltpu.VMEM((width, rows), jnp.bfloat16),
            pltpu.VMEM((width, 128), jnp.float32),
        ],
        compiler_params=params(),
        cost_estimate=pl.CostEstimate(
            flops=3 * rows * width * hidden,
            bytes_accessed=4 * width * hidden,
            transcendentals=0,
        ),
    )(*[blocks[step] for step in steps], gains, *ups)


def late_kernel(tokens, steps, layer, last, *refs):
    count = len(steps)
    block_refs = refs[:count]
    early_ref, gain_ref, up_a, up_b, down_a, down_b = refs[count : count + 6]
    out_refs = refs[count + 6 : -3]
    turned_ref, column_ref, total_ref = refs[-3:]
    width = turned_ref.shape[0]
    load_blocks(steps, block_refs, turned_ref)
    gain_column(layer, gain_ref, column_ref)
    latest = quarters(tokens, layer)[-1]
    part = gained(tokens, latest, turned_ref, column_ref)
    values = turned_ref[...].T.astype(jnp.float32)
    mean = jnp.mean(values * values, axis=-1, keepdims=True)
    scale = lax.rsqrt(mean + EPS)
    total_ref[...] = values
    for half, (up, down) in enumerate(((up_a, down_a), (up_b, down_b))):
        for tile in tiles(up.shape[-1]):
            rows = quarter_rows(tokens, width, latest)
            hidden = jnp.dot(
                part, up[layer, 0, rows, tile], preferred_element_type=jnp.float32
            )
            hidden = gelu((hidden + early_ref[half, :, tile]) * scale)
            total_ref[...] += jnp.dot(
                hidden.astype(jnp.bfloat16),
                down[layer, 0, tile, :],
                preferred_element_type=jnp.float32,
            )
    state = total_ref[...].astype(jnp.bfloat16)
    if last:
        out_refs[0][0] = state
    else:
        turned_ref[...] = state.T
        store_blocks(range(tokens), turned_ref, out_refs)


def late(blocks, begun, gains, ups, downs, layer, last):
    height, rows = blocks[0].shape
    width, hidden = ups[0].shape[2:]
    tokens = width // height
    steps = [0, *order(tokens, layer)]
    if last:
        out_shape = [jax.ShapeDtypeStruct((1, rows, width), jnp.bfloat16)]
    else:
        out_shape = [jax.ShapeDtypeStruct((height, rows), jnp.bfloat16)] * tokens
    return pl.pallas_call(
        functools.partial(late_kernel, tokens, steps, layer, last),
        in_specs=[IN_VMEM] * (tokens + 6),
        out_specs=[IN_VMEM] * len(out_shape),
        out_shape=out_shape,
        scratch_shapes=[
            pltpu.VMEM((width, rows), jnp.bfloat16),
            pltpu.VMEM((width, 128), jnp.float32),
            pltpu.VMEM((rows, width), jnp.float32),
        ],
        compiler_params=params(),
        cost_estimate=pl.CostEstimate(
            flops=5 * rows * width * hidden,
            bytes_accessed=8 * width * hidden,
            transcendentals=2 * rows * hidden,
        ),
    )(*[blocks[step] for step in steps], begun, gains, *ups, *downs)


def exchange(blocks, layer):
    tokens = len(blocks)
    received = [blocks[0]] + [None] * (tokens - 1)
    for step in order(tokens, layer):
        pairs = [
            (2 * t + h, 2 * (t ^ step) + h) for t in range(tokens) for h in range(2)
        ]
        received[step] = lax.ppermute(blocks[step], "tok", pairs)
    return received


def shards(features, w_up, w_down, gains):
    count = lax.axis_size("tok")
    tokens = count // 2
    pairs = [(i, i ^ 1) for i in range(count)]
    ups = (w_up, lax.ppermute(w_up, "tok", pairs))
    downs = (w_down, lax.ppermute(w_down, "tok", pairs))
    blocks = split(features, tokens)
    layers = w_up.shape[0]
    for layer in range(layers):
        blocks = exchange(blocks, layer)
        begun = early(blocks, gains, ups, layer)
        blocks = late(blocks, begun, gains, ups, downs, layer, layer == layers - 1)
    return blocks[0]


def solution(mesh):
    placed = (P("tok", "groups", None), P(None, "tok", None, None), P(None, "tok", None, None), P())
    return jax.shard_map(
        shards, mesh=mesh, in_specs=placed, out_specs=P("tok", "groups", None), check_vma=False
    )
```

```python
import functools

import jax
import jax.numpy as jnp
from jax import lax
from jax.experimental import pallas as pl
from jax.experimental.pallas import tpu as pltpu
from jax.sharding import PartitionSpec as P

EPS = 1e-06
CUBIC = 0.044715
ROOT = 0.7978845608028654
VMEM_LIMIT = 16 << 20
TILE = 768
IN_VMEM = pl.BlockSpec(memory_space=pltpu.VMEM)


def params():
    return pltpu.CompilerParams(vmem_limit_bytes=VMEM_LIMIT)


def order(tokens, layer):
    half, quarter = tokens // 2, tokens // 4
    near = list(range(1, half))
    third, fourth = (
        list(range(start, start + quarter)) for start in (half, half + quarter)
    )
    if layer == 0:
        first, second, latest = near, fourth, third
    else:
        near.sort(key=lambda step: step != 2)
        first, second, latest = third, near, fourth
    mixed = []
    while first or second:
        mixed += first[:1] + second[:1]
        first, second = first[1:], second[1:]
    return mixed + latest


def this_token():
    return lax.axis_index("tok") // 2


def block_rows(step, height):
    return pl.ds(pl.multiple_of((this_token() ^ step) * height, height), height)


def store_blocks(steps, turned_ref, out_refs):
    for step, out_ref in zip(steps, out_refs):
        out_ref[...] = turned_ref[block_rows(step, out_ref.shape[0]), :]


def load_blocks(steps, block_refs, turned_ref):
    for step, ref in zip(steps, block_refs):
        turned_ref[block_rows(step, ref.shape[0]), :] = ref[...]


def split_kernel(tokens, x_ref, *refs):
    *out_refs, turned_ref = refs
    turned_ref[...] = x_ref[0].T
    store_blocks(range(tokens), turned_ref, out_refs)


def split(features, tokens):
    _, rows, width = features.shape
    block = jax.ShapeDtypeStruct((width // tokens, rows), features.dtype)
    return pl.pallas_call(
        functools.partial(split_kernel, tokens),
        in_specs=[IN_VMEM],
        out_specs=[IN_VMEM] * tokens,
        out_shape=[block] * tokens,
        scratch_shapes=[pltpu.VMEM((width, rows), features.dtype)],
        compiler_params=params(),
        cost_estimate=pl.CostEstimate(
            flops=20000000000, bytes_accessed=4 * rows * width, transcendentals=0
        ),
    )(features)


def gelu(v):
    half = 0.5 * v
    return half + half * jnp.tanh(v * (ROOT + (ROOT * CUBIC) * (v * v)))


def spans(tokens, width, layer):
    size, count = width // 4, tokens // 4
    latest = order(tokens, layer)[-1] // count
    starts = [
        pl.multiple_of((this_token() // count ^ which) * size, size)
        for which in [which for which in range(4) if which != latest] + [latest]
    ]
    cut = size * 2 // 3
    early = [pl.ds(starts[0], size), pl.ds(starts[1], size), pl.ds(starts[2], cut)]
    rest = pl.ds(pl.multiple_of(starts[2] + cut, size - cut), size - cut)
    return early, [pl.ds(starts[3], size), rest]


def gained(rows, turned_ref, column_ref):
    values = [
        (turned_ref[span, :].astype(jnp.float32) * column_ref[span, :1]).astype(
            jnp.bfloat16
        )
        for span in rows
    ]
    return jnp.concatenate(values, axis=0).T


def projected(part, up_ref, layer, rows, tile):
    weights = [up_ref[layer, 0, span, tile] for span in rows]
    return jnp.dot(
        part, jnp.concatenate(weights, axis=0), preferred_element_type=jnp.float32
    )


def gain_column(layer, gain_ref, column_ref):
    gain = gain_ref[layer, pl.ds(this_token(), 1), :]
    column_ref[...] = jnp.broadcast_to(gain, column_ref.shape[::-1]).T


def tiles(size):
    tile = TILE if size % TILE == 0 else size
    return [slice(start, start + tile) for start in range(0, size, tile)]


def early_kernel(tokens, steps, layer, *refs):
    count = len(steps)
    block_refs = refs[:count]
    gain_ref, *up_refs, out_ref, turned_ref, column_ref = refs[count:]
    width = turned_ref.shape[0]
    load_blocks(steps, block_refs, turned_ref)
    gain_column(layer, gain_ref, column_ref)
    rows, _ = spans(tokens, width, layer)
    part = gained(rows, turned_ref, column_ref)
    for half, up_ref in enumerate(up_refs):
        for tile in tiles(up_ref.shape[-1]):
            out_ref[half, :, tile] = projected(part, up_ref, layer, rows, tile)


def early(blocks, gains, ups, layer):
    height, rows = blocks[0].shape
    width, hidden = ups[0].shape[2:]
    tokens = width // height
    steps = [*order(tokens, layer)[: -(tokens // 4)], 0]
    return pl.pallas_call(
        functools.partial(early_kernel, tokens, steps, layer),
        in_specs=[IN_VMEM] * (len(steps) + 3),
        out_specs=IN_VMEM,
        out_shape=jax.ShapeDtypeStruct((2, rows, hidden), jnp.float32),
        scratch_shapes=[
            pltpu.VMEM((width, rows), jnp.bfloat16),
            pltpu.VMEM((width, 128), jnp.float32),
        ],
        compiler_params=params(),
        cost_estimate=pl.CostEstimate(
            flops=3 * rows * width * hidden,
            bytes_accessed=4 * width * hidden,
            transcendentals=0,
        ),
    )(*[blocks[step] for step in steps], gains, *ups)


def late_kernel(tokens, steps, layer, last, *refs):
    count = len(steps)
    block_refs = refs[:count]
    early_ref, gain_ref, up_a, up_b, down_a, down_b = refs[count : count + 6]
    out_refs = refs[count + 6 : -3]
    turned_ref, column_ref, total_ref = refs[-3:]
    width = turned_ref.shape[0]
    load_blocks(steps, block_refs, turned_ref)
    gain_column(layer, gain_ref, column_ref)
    _, rows = spans(tokens, width, layer)
    part = gained(rows, turned_ref, column_ref)
    values = turned_ref[...].T.astype(jnp.float32)
    mean = jnp.mean(values * values, axis=-1, keepdims=True)
    scale = lax.rsqrt(mean + EPS)
    total_ref[...] = values
    for half, (up, down) in enumerate(((up_a, down_a), (up_b, down_b))):
        for tile in tiles(up.shape[-1]):
            hidden = projected(part, up, layer, rows, tile)
            hidden = gelu((hidden + early_ref[half, :, tile]) * scale)
            total_ref[...] += jnp.dot(
                hidden.astype(jnp.bfloat16),
                down[layer, 0, tile, :],
                preferred_element_type=jnp.float32,
            )
    state = total_ref[...].astype(jnp.bfloat16)
    if last:
        out_refs[0][0] = state
    else:
        turned_ref[...] = state.T
        store_blocks(range(tokens), turned_ref, out_refs)


def late(blocks, begun, gains, ups, downs, layer, last):
    height, rows = blocks[0].shape
    width, hidden = ups[0].shape[2:]
    tokens = width // height
    steps = [0, *order(tokens, layer)]
    if last:
        out_shape = [jax.ShapeDtypeStruct((1, rows, width), jnp.bfloat16)]
    else:
        out_shape = [jax.ShapeDtypeStruct((height, rows), jnp.bfloat16)] * tokens
    return pl.pallas_call(
        functools.partial(late_kernel, tokens, steps, layer, last),
        in_specs=[IN_VMEM] * (tokens + 6),
        out_specs=[IN_VMEM] * len(out_shape),
        out_shape=out_shape,
        scratch_shapes=[
            pltpu.VMEM((width, rows), jnp.bfloat16),
            pltpu.VMEM((width, 128), jnp.float32),
            pltpu.VMEM((rows, width), jnp.float32),
        ],
        compiler_params=params(),
        cost_estimate=pl.CostEstimate(
            flops=5 * rows * width * hidden,
            bytes_accessed=8 * width * hidden,
            transcendentals=2 * rows * hidden,
        ),
    )(*[blocks[step] for step in steps], begun, gains, *ups, *downs)


def exchange(blocks, layer):
    tokens = len(blocks)
    received = [blocks[0]] + [None] * (tokens - 1)
    for step in order(tokens, layer):
        pairs = [
            (2 * t + h, 2 * (t ^ step) + h) for t in range(tokens) for h in range(2)
        ]
        received[step] = lax.ppermute(blocks[step], "tok", pairs)
    return received


def shards(features, w_up, w_down, gains):
    count = lax.axis_size("tok")
    tokens = count // 2
    pairs = [(i, i ^ 1) for i in range(count)]
    ups = (w_up, lax.ppermute(w_up, "tok", pairs))
    downs = (w_down, lax.ppermute(w_down, "tok", pairs))
    blocks = split(features, tokens)
    layers = w_up.shape[0]
    for layer in range(layers):
        blocks = exchange(blocks, layer)
        begun = early(blocks, gains, ups, layer)
        blocks = late(blocks, begun, gains, ups, downs, layer, layer == layers - 1)
    return blocks[0]


def solution(mesh):
    placed = (P("tok", "groups", None), P(None, "tok", None, None), P(None, "tok", None, None), P())
    return jax.shard_map(
        shards, mesh=mesh, in_specs=placed, out_specs=P("tok", "groups", None), check_vma=False
    )
```

```python
import functools

import jax
import jax.numpy as jnp
from jax import lax
from jax.experimental import pallas as pl
from jax.experimental.pallas import tpu as pltpu
from jax.sharding import PartitionSpec as P

EPS = 1e-06
CUBIC = 0.044715
ROOT = 0.7978845608028654
VMEM_LIMIT = 16 << 20
TILE = 512
IN_VMEM = pl.BlockSpec(memory_space=pltpu.VMEM)


def params():
    return pltpu.CompilerParams(vmem_limit_bytes=VMEM_LIMIT)


def order(tokens, layer):
    half, quarter = tokens // 2, tokens // 4
    near = list(range(1, half))
    third, fourth = (
        list(range(start, start + quarter)) for start in (half, half + quarter)
    )
    if layer == 0:
        first, second, latest = near, fourth, third
    else:
        near.sort(key=lambda step: step != 2)
        first, second, latest = third, near, fourth
    mixed = []
    while first or second:
        mixed += first[:1] + second[:1]
        first, second = first[1:], second[1:]
    return mixed + latest


def this_token():
    return lax.axis_index("tok") // 2


def block_rows(step, height):
    return pl.ds(pl.multiple_of((this_token() ^ step) * height, height), height)


def store_blocks(steps, turned_ref, out_refs):
    for step, out_ref in zip(steps, out_refs):
        out_ref[...] = turned_ref[block_rows(step, out_ref.shape[0]), :]


def load_blocks(steps, block_refs, turned_ref):
    for step, ref in zip(steps, block_refs):
        turned_ref[block_rows(step, ref.shape[0]), :] = ref[...]


def split_kernel(tokens, x_ref, *refs):
    *out_refs, turned_ref = refs
    turned_ref[...] = x_ref[0].T
    store_blocks(range(tokens), turned_ref, out_refs)


def split(features, tokens):
    _, rows, width = features.shape
    block = jax.ShapeDtypeStruct((width // tokens, rows), features.dtype)
    return pl.pallas_call(
        functools.partial(split_kernel, tokens),
        in_specs=[IN_VMEM],
        out_specs=[IN_VMEM] * tokens,
        out_shape=[block] * tokens,
        scratch_shapes=[pltpu.VMEM((width, rows), features.dtype)],
        compiler_params=params(),
        cost_estimate=pl.CostEstimate(
            flops=20000000000, bytes_accessed=4 * rows * width, transcendentals=0
        ),
    )(features)


def gelu(v):
    half = 0.5 * v
    return half + half * jnp.tanh(v * (ROOT + (ROOT * CUBIC) * (v * v)))


def spans(tokens, width, layer):
    size, count = width // 4, tokens // 4
    latest = order(tokens, layer)[-1] // count
    starts = [
        pl.multiple_of((this_token() // count ^ which) * size, size)
        for which in [which for which in range(4) if which != latest] + [latest]
    ]
    cut = size * 2 // 3
    early = [pl.ds(starts[0], size), pl.ds(starts[1], size), pl.ds(starts[2], cut)]
    rest = pl.ds(pl.multiple_of(starts[2] + cut, size - cut), size - cut)
    return early, [pl.ds(starts[3], size), rest]


def gained(rows, turned_ref, column_ref):
    values = [
        (turned_ref[span, :].astype(jnp.float32) * column_ref[span, :1]).astype(
            jnp.bfloat16
        )
        for span in rows
    ]
    return jnp.concatenate(values, axis=0).T


def projected(part, up_ref, layer, rows, tile):
    weights = [up_ref[layer, 0, span, tile] for span in rows]
    return jnp.dot(
        part, jnp.concatenate(weights, axis=0), preferred_element_type=jnp.float32
    )


def gain_column(layer, gain_ref, column_ref):
    gain = gain_ref[layer, pl.ds(this_token(), 1), :]
    column_ref[...] = jnp.broadcast_to(gain, column_ref.shape[::-1]).T


def tiles(size):
    tile = TILE if size % TILE == 0 else size
    return [slice(start, start + tile) for start in range(0, size, tile)]


def early_kernel(tokens, steps, layer, *refs):
    count = len(steps)
    block_refs = refs[:count]
    gain_ref, *up_refs, out_ref, turned_ref, column_ref = refs[count:]
    width = turned_ref.shape[0]
    load_blocks(steps, block_refs, turned_ref)
    gain_column(layer, gain_ref, column_ref)
    rows, _ = spans(tokens, width, layer)
    part = gained(rows, turned_ref, column_ref)
    for half, up_ref in enumerate(up_refs):
        for tile in tiles(up_ref.shape[-1]):
            out_ref[half, :, tile] = projected(part, up_ref, layer, rows, tile)


def early(blocks, gains, ups, layer):
    height, rows = blocks[0].shape
    width, hidden = ups[0].shape[2:]
    tokens = width // height
    steps = [*order(tokens, layer)[: -(tokens // 4)], 0]
    return pl.pallas_call(
        functools.partial(early_kernel, tokens, steps, layer),
        in_specs=[IN_VMEM] * (len(steps) + 3),
        out_specs=IN_VMEM,
        out_shape=jax.ShapeDtypeStruct((2, rows, hidden), jnp.float32),
        scratch_shapes=[
            pltpu.VMEM((width, rows), jnp.bfloat16),
            pltpu.VMEM((width, 128), jnp.float32),
        ],
        compiler_params=params(),
        cost_estimate=pl.CostEstimate(
            flops=3 * rows * width * hidden,
            bytes_accessed=4 * width * hidden,
            transcendentals=0,
        ),
    )(*[blocks[step] for step in steps], gains, *ups)


def late_kernel(tokens, steps, layer, last, *refs):
    count = len(steps)
    block_refs = refs[:count]
    early_ref, gain_ref, up_a, up_b, down_a, down_b = refs[count : count + 6]
    out_refs = refs[count + 6 : -3]
    turned_ref, column_ref, total_ref = refs[-3:]
    width = turned_ref.shape[0]
    load_blocks(steps, block_refs, turned_ref)
    gain_column(layer, gain_ref, column_ref)
    _, rows = spans(tokens, width, layer)
    part = gained(rows, turned_ref, column_ref)
    values = turned_ref[...].T.astype(jnp.float32)
    mean = jnp.mean(values * values, axis=-1, keepdims=True)
    scale = lax.rsqrt(mean + EPS)
    total_ref[...] = values
    for half, (up, down) in enumerate(((up_a, down_a), (up_b, down_b))):
        for tile in tiles(up.shape[-1]):
            hidden = projected(part, up, layer, rows, tile)
            hidden = gelu((hidden + early_ref[half, :, tile]) * scale)
            total_ref[...] += jnp.dot(
                hidden.astype(jnp.bfloat16),
                down[layer, 0, tile, :],
                preferred_element_type=jnp.float32,
            )
    state = total_ref[...].astype(jnp.bfloat16)
    if last:
        out_refs[0][0] = state
    else:
        turned_ref[...] = state.T
        store_blocks(range(tokens), turned_ref, out_refs)


def late(blocks, begun, gains, ups, downs, layer, last):
    height, rows = blocks[0].shape
    width, hidden = ups[0].shape[2:]
    tokens = width // height
    steps = [0, *order(tokens, layer)]
    if last:
        out_shape = [jax.ShapeDtypeStruct((1, rows, width), jnp.bfloat16)]
    else:
        out_shape = [jax.ShapeDtypeStruct((height, rows), jnp.bfloat16)] * tokens
    return pl.pallas_call(
        functools.partial(late_kernel, tokens, steps, layer, last),
        in_specs=[IN_VMEM] * (tokens + 6),
        out_specs=[IN_VMEM] * len(out_shape),
        out_shape=out_shape,
        scratch_shapes=[
            pltpu.VMEM((width, rows), jnp.bfloat16),
            pltpu.VMEM((width, 128), jnp.float32),
            pltpu.VMEM((rows, width), jnp.float32),
        ],
        compiler_params=params(),
        cost_estimate=pl.CostEstimate(
            flops=5 * rows * width * hidden,
            bytes_accessed=8 * width * hidden,
            transcendentals=2 * rows * hidden,
        ),
    )(*[blocks[step] for step in steps], begun, gains, *ups, *downs)


def exchange(blocks, layer):
    tokens = len(blocks)
    received = [blocks[0]] + [None] * (tokens - 1)
    for step in order(tokens, layer):
        pairs = [
            (2 * t + h, 2 * (t ^ step) + h) for t in range(tokens) for h in range(2)
        ]
        received[step] = lax.ppermute(blocks[step], "tok", pairs)
    return received


def shards(features, w_up, w_down, gains):
    count = lax.axis_size("tok")
    tokens = count // 2
    pairs = [(i, i ^ 1) for i in range(count)]
    ups = (w_up, lax.ppermute(w_up, "tok", pairs))
    downs = (w_down, lax.ppermute(w_down, "tok", pairs))
    blocks = split(features, tokens)
    layers = w_up.shape[0]
    for layer in range(layers):
        blocks = exchange(blocks, layer)
        begun = early(blocks, gains, ups, layer)
        blocks = late(blocks, begun, gains, ups, downs, layer, layer == layers - 1)
    return blocks[0]


def solution(mesh):
    placed = (P("tok", "groups", None), P(None, "tok", None, None), P(None, "tok", None, None), P())
    return jax.shard_map(
        shards, mesh=mesh, in_specs=placed, out_specs=P("tok", "groups", None), check_vma=False
    )
```

```python
import functools

import jax
import jax.numpy as jnp
from jax import lax
from jax.experimental import pallas as pl
from jax.experimental.pallas import tpu as pltpu
from jax.sharding import PartitionSpec as P

EPS = 1e-06
CUBIC = 0.044715
ROOT = 0.7978845608028654
VMEM_LIMIT = 16 << 20
TILE = 512
IN_VMEM = pl.BlockSpec(memory_space=pltpu.VMEM)


def params():
    return pltpu.CompilerParams(vmem_limit_bytes=VMEM_LIMIT)


def order(tokens, layer):
    half, quarter = tokens // 2, tokens // 4
    near = list(range(1, half))
    third, fourth = (
        list(range(start, start + quarter)) for start in (half, half + quarter)
    )
    if layer == 0:
        first, second, latest = near, fourth, third
    else:
        first, second, latest = third, near[1:] + near[:1], fourth
    mixed = []
    while first or second:
        mixed += first[:1] + second[:1]
        first, second = first[1:], second[1:]
    return mixed + latest[::-1]


def this_token():
    return lax.axis_index("tok") // 2


def block_rows(step, height):
    return pl.ds(pl.multiple_of((this_token() ^ step) * height, height), height)


def store_blocks(steps, turned_ref, out_refs):
    for step, out_ref in zip(steps, out_refs):
        out_ref[...] = turned_ref[block_rows(step, out_ref.shape[0]), :]


def load_blocks(steps, block_refs, turned_ref):
    for step, ref in zip(steps, block_refs):
        turned_ref[block_rows(step, ref.shape[0]), :] = ref[...]


def split_kernel(tokens, x_ref, *refs):
    *out_refs, turned_ref = refs
    turned_ref[...] = x_ref[0].T
    store_blocks(range(tokens), turned_ref, out_refs)


def split(features, tokens):
    _, rows, width = features.shape
    block = jax.ShapeDtypeStruct((width // tokens, rows), features.dtype)
    return pl.pallas_call(
        functools.partial(split_kernel, tokens),
        in_specs=[IN_VMEM],
        out_specs=[IN_VMEM] * tokens,
        out_shape=[block] * tokens,
        scratch_shapes=[pltpu.VMEM((width, rows), features.dtype)],
        compiler_params=params(),
        cost_estimate=pl.CostEstimate(
            flops=20000000000, bytes_accessed=4 * rows * width, transcendentals=0
        ),
    )(features)


def gelu(v):
    half = 0.5 * v
    return half + half * jnp.tanh(v * (ROOT + (ROOT * CUBIC) * (v * v)))


def spans(tokens, width, layer):
    size, count = width // 4, tokens // 4
    latest = order(tokens, layer)[-1] // count
    starts = [
        pl.multiple_of((this_token() // count ^ which) * size, size)
        for which in [which for which in range(4) if which != latest] + [latest]
    ]
    cut = size * 2 // 3
    early = [pl.ds(starts[0], size), pl.ds(starts[1], size), pl.ds(starts[2], cut)]
    rest = pl.ds(pl.multiple_of(starts[2] + cut, size - cut), size - cut)
    return early, [pl.ds(starts[3], size), rest]


def gained(rows, turned_ref, column_ref):
    values = [
        (turned_ref[span, :].astype(jnp.float32) * column_ref[span, :1]).astype(
            jnp.bfloat16
        )
        for span in rows
    ]
    return jnp.concatenate(values, axis=0).T


def projected(part, up_ref, layer, rows, tile):
    weights = [up_ref[layer, 0, span, tile] for span in rows]
    return jnp.dot(
        part, jnp.concatenate(weights, axis=0), preferred_element_type=jnp.float32
    )


def gain_column(layer, gain_ref, column_ref):
    gain = gain_ref[layer, pl.ds(this_token(), 1), :]
    column_ref[...] = jnp.broadcast_to(gain, column_ref.shape[::-1]).T


def tiles(size):
    tile = TILE if size % TILE == 0 else size
    return [slice(start, start + tile) for start in range(0, size, tile)]


def early_kernel(tokens, steps, layer, *refs):
    count = len(steps)
    block_refs = refs[:count]
    gain_ref, *up_refs, out_ref, turned_ref, column_ref = refs[count:]
    width = turned_ref.shape[0]
    load_blocks(steps, block_refs, turned_ref)
    gain_column(layer, gain_ref, column_ref)
    rows, _ = spans(tokens, width, layer)
    part = gained(rows, turned_ref, column_ref)
    for half, up_ref in enumerate(up_refs):
        for tile in tiles(up_ref.shape[-1]):
            out_ref[half, :, tile] = projected(part, up_ref, layer, rows, tile)


def early(blocks, gains, ups, layer):
    height, rows = blocks[0].shape
    width, hidden = ups[0].shape[2:]
    tokens = width // height
    steps = [*order(tokens, layer)[: -(tokens // 4)], 0]
    return pl.pallas_call(
        functools.partial(early_kernel, tokens, steps, layer),
        in_specs=[IN_VMEM] * (len(steps) + 3),
        out_specs=IN_VMEM,
        out_shape=jax.ShapeDtypeStruct((2, rows, hidden), jnp.float32),
        scratch_shapes=[
            pltpu.VMEM((width, rows), jnp.bfloat16),
            pltpu.VMEM((width, 128), jnp.float32),
        ],
        compiler_params=params(),
        cost_estimate=pl.CostEstimate(
            flops=3 * rows * width * hidden,
            bytes_accessed=4 * width * hidden,
            transcendentals=0,
        ),
    )(*[blocks[step] for step in steps], gains, *ups)


def late_kernel(tokens, steps, layer, last, *refs):
    count = len(steps)
    block_refs = refs[:count]
    early_ref, gain_ref, up_a, up_b, down_a, down_b = refs[count : count + 6]
    out_refs = refs[count + 6 : -3]
    turned_ref, column_ref, total_ref = refs[-3:]
    width = turned_ref.shape[0]
    load_blocks(steps, block_refs, turned_ref)
    gain_column(layer, gain_ref, column_ref)
    _, rows = spans(tokens, width, layer)
    part = gained(rows, turned_ref, column_ref)
    values = turned_ref[...].T.astype(jnp.float32)
    mean = jnp.mean(values * values, axis=-1, keepdims=True)
    scale = lax.rsqrt(mean + EPS)
    total_ref[...] = values
    for half, (up, down) in enumerate(((up_a, down_a), (up_b, down_b))):
        for tile in tiles(up.shape[-1]):
            hidden = projected(part, up, layer, rows, tile)
            hidden = gelu((hidden + early_ref[half, :, tile]) * scale)
            total_ref[...] += jnp.dot(
                hidden.astype(jnp.bfloat16),
                down[layer, 0, tile, :],
                preferred_element_type=jnp.float32,
            )
    state = total_ref[...].astype(jnp.bfloat16)
    if last:
        out_refs[0][0] = state
    else:
        turned_ref[...] = state.T
        store_blocks(range(tokens), turned_ref, out_refs)


def late(blocks, begun, gains, ups, downs, layer, last):
    height, rows = blocks[0].shape
    width, hidden = ups[0].shape[2:]
    tokens = width // height
    steps = [0, *order(tokens, layer)]
    if last:
        out_shape = [jax.ShapeDtypeStruct((1, rows, width), jnp.bfloat16)]
    else:
        out_shape = [jax.ShapeDtypeStruct((height, rows), jnp.bfloat16)] * tokens
    return pl.pallas_call(
        functools.partial(late_kernel, tokens, steps, layer, last),
        in_specs=[IN_VMEM] * (tokens + 6),
        out_specs=[IN_VMEM] * len(out_shape),
        out_shape=out_shape,
        scratch_shapes=[
            pltpu.VMEM((width, rows), jnp.bfloat16),
            pltpu.VMEM((width, 128), jnp.float32),
            pltpu.VMEM((rows, width), jnp.float32),
        ],
        compiler_params=params(),
        cost_estimate=pl.CostEstimate(
            flops=5 * rows * width * hidden,
            bytes_accessed=8 * width * hidden,
            transcendentals=2 * rows * hidden,
        ),
    )(*[blocks[step] for step in steps], begun, gains, *ups, *downs)


def exchange(blocks, layer):
    tokens = len(blocks)
    received = [blocks[0]] + [None] * (tokens - 1)
    for step in order(tokens, layer):
        pairs = [
            (2 * t + h, 2 * (t ^ step) + h) for t in range(tokens) for h in range(2)
        ]
        received[step] = lax.ppermute(blocks[step], "tok", pairs)
    return received


def shards(features, w_up, w_down, gains):
    count = lax.axis_size("tok")
    tokens = count // 2
    pairs = [(i, i ^ 1) for i in range(count)]
    ups = (w_up, lax.ppermute(w_up, "tok", pairs))
    downs = (w_down, lax.ppermute(w_down, "tok", pairs))
    blocks = split(features, tokens)
    layers = w_up.shape[0]
    for layer in range(layers):
        blocks = exchange(blocks, layer)
        begun = early(blocks, gains, ups, layer)
        blocks = late(blocks, begun, gains, ups, downs, layer, layer == layers - 1)
    return blocks[0]


def solution(mesh):
    placed = (P("tok", "groups", None), P(None, "tok", None, None), P(None, "tok", None, None), P())
    return jax.shard_map(
        shards, mesh=mesh, in_specs=placed, out_specs=P("tok", "groups", None), check_vma=False
    )
```

```python
import functools

import jax
import jax.numpy as jnp
from jax import lax
from jax.experimental import pallas as pl
from jax.experimental.pallas import tpu as pltpu
from jax.sharding import PartitionSpec as P

EPS = 1e-06
CUBIC = 0.044715
ROOT = 0.7978845608028654
VMEM_LIMIT = 16 << 20
TILE = 512
IN_VMEM = pl.BlockSpec(memory_space=pltpu.VMEM)


def params():
    return pltpu.CompilerParams(vmem_limit_bytes=VMEM_LIMIT)


def order(tokens, layer):
    half, quarter = tokens // 2, tokens // 4
    near = list(range(1, half))
    third, fourth = (
        list(range(start, start + quarter)) for start in (half, half + quarter)
    )
    if layer == 0:
        first, second, latest = near, fourth, third
    else:
        first, second, latest = third, near[::-1], fourth
    mixed = []
    while first or second:
        mixed += first[:1] + second[:1]
        first, second = first[1:], second[1:]
    return mixed + latest[::-1]


def this_token():
    return lax.axis_index("tok") // 2


def block_rows(step, height):
    return pl.ds(pl.multiple_of((this_token() ^ step) * height, height), height)


def store_blocks(steps, turned_ref, out_refs):
    for step, out_ref in zip(steps, out_refs):
        out_ref[...] = turned_ref[block_rows(step, out_ref.shape[0]), :]


def load_blocks(steps, block_refs, turned_ref):
    for step, ref in zip(steps, block_refs):
        turned_ref[block_rows(step, ref.shape[0]), :] = ref[...]


def split_kernel(tokens, x_ref, *refs):
    *out_refs, turned_ref = refs
    turned_ref[...] = x_ref[0].T
    store_blocks(range(tokens), turned_ref, out_refs)


def split(features, tokens):
    _, rows, width = features.shape
    block = jax.ShapeDtypeStruct((width // tokens, rows), features.dtype)
    return pl.pallas_call(
        functools.partial(split_kernel, tokens),
        in_specs=[IN_VMEM],
        out_specs=[IN_VMEM] * tokens,
        out_shape=[block] * tokens,
        scratch_shapes=[pltpu.VMEM((width, rows), features.dtype)],
        compiler_params=params(),
        cost_estimate=pl.CostEstimate(
            flops=20000000000, bytes_accessed=4 * rows * width, transcendentals=0
        ),
    )(features)


def gelu(v):
    half = 0.5 * v
    return half + half * jnp.tanh(v * (ROOT + (ROOT * CUBIC) * (v * v)))


def spans(tokens, width, layer):
    size, count = width // 4, tokens // 4
    latest = order(tokens, layer)[-1] // count
    starts = [
        pl.multiple_of((this_token() // count ^ which) * size, size)
        for which in [which for which in range(4) if which != latest] + [latest]
    ]
    cut = size * 2 // 3
    early = [pl.ds(starts[0], size), pl.ds(starts[1], size), pl.ds(starts[2], cut)]
    rest = pl.ds(pl.multiple_of(starts[2] + cut, size - cut), size - cut)
    return early, [pl.ds(starts[3], size), rest]


def gained(rows, turned_ref, column_ref):
    values = [
        (turned_ref[span, :].astype(jnp.float32) * column_ref[span, :1]).astype(
            jnp.bfloat16
        )
        for span in rows
    ]
    return jnp.concatenate(values, axis=0).T


def projected(part, up_ref, layer, rows, tile):
    weights = [up_ref[layer, 0, span, tile] for span in rows]
    return jnp.dot(
        part, jnp.concatenate(weights, axis=0), preferred_element_type=jnp.float32
    )


def gain_column(layer, gain_ref, column_ref):
    gain = gain_ref[layer, pl.ds(this_token(), 1), :]
    column_ref[...] = jnp.broadcast_to(gain, column_ref.shape[::-1]).T


def tiles(size):
    tile = TILE if size % TILE == 0 else size
    return [slice(start, start + tile) for start in range(0, size, tile)]


def early_kernel(tokens, steps, layer, *refs):
    count = len(steps)
    block_refs = refs[:count]
    gain_ref, *up_refs, out_ref, turned_ref, column_ref = refs[count:]
    width = turned_ref.shape[0]
    load_blocks(steps, block_refs, turned_ref)
    gain_column(layer, gain_ref, column_ref)
    rows, _ = spans(tokens, width, layer)
    part = gained(rows, turned_ref, column_ref)
    for half, up_ref in enumerate(up_refs):
        for tile in tiles(up_ref.shape[-1]):
            out_ref[half, :, tile] = projected(part, up_ref, layer, rows, tile)


def early(blocks, gains, ups, layer):
    height, rows = blocks[0].shape
    width, hidden = ups[0].shape[2:]
    tokens = width // height
    steps = [*order(tokens, layer)[: -(tokens // 4)], 0]
    return pl.pallas_call(
        functools.partial(early_kernel, tokens, steps, layer),
        in_specs=[IN_VMEM] * (len(steps) + 3),
        out_specs=IN_VMEM,
        out_shape=jax.ShapeDtypeStruct((2, rows, hidden), jnp.float32),
        scratch_shapes=[
            pltpu.VMEM((width, rows), jnp.bfloat16),
            pltpu.VMEM((width, 128), jnp.float32),
        ],
        compiler_params=params(),
        cost_estimate=pl.CostEstimate(
            flops=3 * rows * width * hidden,
            bytes_accessed=4 * width * hidden,
            transcendentals=0,
        ),
    )(*[blocks[step] for step in steps], gains, *ups)


def late_kernel(tokens, steps, layer, last, *refs):
    count = len(steps)
    block_refs = refs[:count]
    early_ref, gain_ref, up_a, up_b, down_a, down_b = refs[count : count + 6]
    out_refs = refs[count + 6 : -3]
    turned_ref, column_ref, total_ref = refs[-3:]
    width = turned_ref.shape[0]
    load_blocks(steps, block_refs, turned_ref)
    gain_column(layer, gain_ref, column_ref)
    _, rows = spans(tokens, width, layer)
    part = gained(rows, turned_ref, column_ref)
    values = turned_ref[...].T.astype(jnp.float32)
    mean = jnp.mean(values * values, axis=-1, keepdims=True)
    scale = lax.rsqrt(mean + EPS)
    total_ref[...] = values
    for half, (up, down) in enumerate(((up_a, down_a), (up_b, down_b))):
        for tile in tiles(up.shape[-1]):
            hidden = projected(part, up, layer, rows, tile)
            hidden = gelu((hidden + early_ref[half, :, tile]) * scale)
            total_ref[...] += jnp.dot(
                hidden.astype(jnp.bfloat16),
                down[layer, 0, tile, :],
                preferred_element_type=jnp.float32,
            )
    state = total_ref[...].astype(jnp.bfloat16)
    if last:
        out_refs[0][0] = state
    else:
        turned_ref[...] = state.T
        store_blocks(range(tokens), turned_ref, out_refs)


def late(blocks, begun, gains, ups, downs, layer, last):
    height, rows = blocks[0].shape
    width, hidden = ups[0].shape[2:]
    tokens = width // height
    steps = [0, *order(tokens, layer)]
    if last:
        out_shape = [jax.ShapeDtypeStruct((1, rows, width), jnp.bfloat16)]
    else:
        out_shape = [jax.ShapeDtypeStruct((height, rows), jnp.bfloat16)] * tokens
    return pl.pallas_call(
        functools.partial(late_kernel, tokens, steps, layer, last),
        in_specs=[IN_VMEM] * (tokens + 6),
        out_specs=[IN_VMEM] * len(out_shape),
        out_shape=out_shape,
        scratch_shapes=[
            pltpu.VMEM((width, rows), jnp.bfloat16),
            pltpu.VMEM((width, 128), jnp.float32),
            pltpu.VMEM((rows, width), jnp.float32),
        ],
        compiler_params=params(),
        cost_estimate=pl.CostEstimate(
            flops=5 * rows * width * hidden,
            bytes_accessed=8 * width * hidden,
            transcendentals=2 * rows * hidden,
        ),
    )(*[blocks[step] for step in steps], begun, gains, *ups, *downs)


def exchange(blocks, layer):
    tokens = len(blocks)
    received = [blocks[0]] + [None] * (tokens - 1)
    for step in order(tokens, layer):
        pairs = [
            (2 * t + h, 2 * (t ^ step) + h) for t in range(tokens) for h in range(2)
        ]
        received[step] = lax.ppermute(blocks[step], "tok", pairs)
    return received


def shards(features, w_up, w_down, gains):
    count = lax.axis_size("tok")
    tokens = count // 2
    pairs = [(i, i ^ 1) for i in range(count)]
    ups = (w_up, lax.ppermute(w_up, "tok", pairs))
    downs = (w_down, lax.ppermute(w_down, "tok", pairs))
    blocks = split(features, tokens)
    layers = w_up.shape[0]
    for layer in range(layers):
        blocks = exchange(blocks, layer)
        begun = early(blocks, gains, ups, layer)
        blocks = late(blocks, begun, gains, ups, downs, layer, layer == layers - 1)
    return blocks[0]


def solution(mesh):
    placed = (P("tok", "groups", None), P(None, "tok", None, None), P(None, "tok", None, None), P())
    return jax.shard_map(
        shards, mesh=mesh, in_specs=placed, out_specs=P("tok", "groups", None), check_vma=False
    )
```
